32 devices in a mesh: branch: 4 (over x, core), ty: 2 (over y), tx: 4 (over z).
Axes of the slice: x: 2, y: 2, z: 4, core: 2. Of those that a mesh axis runs over, the one named last changes fastest.
Arguments:
- feat0: bfloat16 [48, 128, 256], P(None, 'ty', 'tx'), may hold values from -6 to 6
- feat1: bfloat16 [96, 64, 128], P(None, 'ty', 'tx'), may hold values from -6 to 6
- feat2: bfloat16 [192, 32, 64], P(None, 'ty', 'tx'), may hold values from -6 to 6
- feat3: bfloat16 [384, 16, 32], P(None, 'ty', 'tx'), may hold values from -6 to 6
- block_w0: bfloat16 [2, 48, 432], replicated, may hold values from -0.3125 to 0.3125
- block_w1: bfloat16 [2, 96, 864], replicated, may hold values from -0.21875 to 0.21875
- block_w2: bfloat16 [2, 192, 1728], replicated, may hold values from -0.15625 to 0.15625
- block_w3: bfloat16 [2, 384, 3456], replicated, may hold values from -0.109375 to 0.109375
- block_b0: float32 [2, 48], replicated, may hold values from -1.8 to 1.8
- block_b1: float32 [2, 96], replicated, may hold values from -1.8 to 1.8
- block_b2: float32 [2, 192], replicated, may hold values from -1.8 to 1.8
- block_b3: float32 [2, 384], replicated, may hold values from -1.8 to 1.8
- up_w1: bfloat16 [1, 48, 96], replicated, may hold values from -0.625 to 0.625
- up_w2: bfloat16 [1, 144, 192], replicated, may hold values from -0.4375 to 0.4375
- up_w3: bfloat16 [1, 336, 384], replicated, may hold values from -0.3125 to 0.3125
- down_mid0: bfloat16 [1, 3, 48, 432], replicated, may hold values from -0.3125 to 0.3125
- down_mid1: bfloat16 [1, 1, 96, 864], replicated, may hold values from -0.21875 to 0.21875
- down_fin0: bfloat16 [1, 672, 432], replicated, may hold values from -0.3125 to 0.3125
- down_fin1: bfloat16 [1, 576, 864], replicated, may hold values from -0.21875 to 0.21875
- down_fin2: bfloat16 [1, 384, 1728], replicated, may hold values from -0.15625 to 0.15625
Outputs:
- joined0: bfloat16 [48, 128, 256], P(None, 'ty', 'tx')
- joined1: bfloat16 [96, 64, 128], P(None, 'ty', 'tx')
- joined2: bfloat16 [192, 32, 64], P(None, 'ty', 'tx')
- joined3: bfloat16 [384, 16, 32], P(None, 'ty', 'tx')
The draws below stay inside these ranges and needn't reach their ends.
All inputs are finite; a program needn't handle non-finite values.
Results may differ from the reference program's by a relative error of at most 0.0095.
Values may be sent and summed in bfloat16 or wider, within the bound.
A program may use at most 128 MiB of HBM per device.

```python
import jax
import jax.numpy as jnp

CHAN = 48
MODULES = 1
BLOCKS = 1
CONVS = 2
HEIGHT = 128
WIDTH = 256


def shard_levels(own_key, shape, split, smallest, top_value):
    level, own = 1.0, jax.random.fold_in(own_key, 6)
    for axis_at, shards_of in split:
        draws = jnp.exp(jax.random.uniform(jax.random.fold_in(own, axis_at), (shards_of,), jnp.float32, smallest / len(split), top_value / len(split)))
        level = level * jnp.repeat(draws, shape[axis_at] // shards_of).reshape([-1 if axis == axis_at else 1 for axis in range(len(shape))])
    return level


def normal_values(rng, dims, scale, most, cuts=(), kind=jnp.bfloat16):
    values = scale * jax.random.normal(rng, dims, jnp.float32)
    if cuts:
        values = values * shard_levels(rng, dims, cuts, -0.22, 0.18)
    return jnp.clip(values, -most, most).astype(kind)


def setup_inputs(seed: int = 0) -> dict:
    key_of = jax.random.split(jax.random.key(seed), 21)
    feat0 = normal_values(key_of[0], (CHAN, HEIGHT, WIDTH), 1.0, 6.0, ((1, 2), (2, 4)))
    feat1 = normal_values(key_of[1], (2 * CHAN, HEIGHT // 2, WIDTH // 2), 1.0, 6.0, ((1, 2), (2, 4)))
    feat2 = normal_values(key_of[2], (4 * CHAN, HEIGHT // 4, WIDTH // 4), 1.0, 6.0, ((1, 2), (2, 4)))
    feat3 = normal_values(key_of[3], (8 * CHAN, HEIGHT // 8, WIDTH // 8), 1.0, 6.0, ((1, 2), (2, 4)))
    block_w0 = normal_values(key_of[4], (CONVS, CHAN, 9 * CHAN), (9 * CHAN) ** -0.5, 0.3125)
    block_w1 = normal_values(key_of[5], (CONVS, 2 * CHAN, 18 * CHAN), (18 * CHAN) ** -0.5, 0.21875)
    block_w2 = normal_values(key_of[6], (CONVS, 4 * CHAN, 36 * CHAN), (36 * CHAN) ** -0.5, 0.15625)
    block_w3 = normal_values(key_of[7], (CONVS, 8 * CHAN, 72 * CHAN), (72 * CHAN) ** -0.5, 0.109375)
    block_b0 = normal_values(key_of[8], (CONVS, CHAN), 0.3, 1.8, (), jnp.float32)
    block_b1 = normal_values(key_of[9], (CONVS, 2 * CHAN), 0.3, 1.8, (), jnp.float32)
    block_b2 = normal_values(key_of[10], (CONVS, 4 * CHAN), 0.3, 1.8, (), jnp.float32)
    block_b3 = normal_values(key_of[11], (CONVS, 8 * CHAN), 0.3, 1.8, (), jnp.float32)
    up_w1 = normal_values(key_of[12], (MODULES, CHAN, 2 * CHAN), (2 * CHAN) ** -0.5, 0.625)
    up_w2 = normal_values(key_of[13], (MODULES, 3 * CHAN, 4 * CHAN), (4 * CHAN) ** -0.5, 0.4375)
    up_w3 = normal_values(key_of[14], (MODULES, 7 * CHAN, 8 * CHAN), (8 * CHAN) ** -0.5, 0.3125)
    down_mid0 = normal_values(key_of[15], (MODULES, 3, CHAN, 9 * CHAN), (9 * CHAN) ** -0.5, 0.3125)
    down_mid1 = normal_values(key_of[16], (MODULES, 1, 2 * CHAN, 18 * CHAN), (18 * CHAN) ** -0.5, 0.21875)
    down_fin0 = normal_values(key_of[17], (MODULES, 14 * CHAN, 9 * CHAN), (9 * CHAN) ** -0.5, 0.3125)
    down_fin1 = normal_values(key_of[18], (MODULES, 12 * CHAN, 18 * CHAN), (18 * CHAN) ** -0.5, 0.21875)
    down_fin2 = normal_values(key_of[19], (MODULES, 8 * CHAN, 36 * CHAN), (36 * CHAN) ** -0.5, 0.15625)
    return {"feat0": feat0, "feat1": feat1, "feat2": feat2, "feat3": feat3, "block_w0": block_w0, "block_w1": block_w1, "block_w2": block_w2, "block_w3": block_w3, "block_b0": block_b0, "block_b1": block_b1, "block_b2": block_b2, "block_b3": block_b3, "up_w1": up_w1, "up_w2": up_w2, "up_w3": up_w3, "down_mid0": down_mid0, "down_mid1": down_mid1, "down_fin0": down_fin0, "down_fin1": down_fin1, "down_fin2": down_fin2}


def convolve(feature, weight, stride):
    channels, height, breadth = feature.shape
    padded = jnp.pad(feature, ((0, 0), (1, 1), (1, 1)))
    out_height = height // stride
    out_breadth = breadth // stride
    running = jnp.zeros((weight.shape[0], out_height * out_breadth), jnp.float32)
    for tap_index in range(9):
        row_tap, col_tap = divmod(tap_index, 3)
        window = padded[:, row_tap:row_tap + stride * (out_height - 1) + 1:stride, col_tap:col_tap + stride * (out_breadth - 1) + 1:stride]
        window = window.reshape(channels, out_height * out_breadth)
        running = running + jnp.dot(weight[:, tap_index * channels:(tap_index + 1) * channels], window, preferred_element_type=jnp.float32)
    return running.reshape(weight.shape[0], out_height, out_breadth)


def residual_block(feature, first_weight, first_bias, second_weight, second_bias):
    inner = jax.nn.relu(convolve(feature, first_weight, 1) + first_bias[:, None, None]).astype(jnp.bfloat16)
    summed = feature.astype(jnp.float32) + convolve(inner, second_weight, 1) + second_bias[:, None, None]
    return jax.nn.relu(summed).astype(jnp.bfloat16)


def joining_terms(source, source_id, module_id, channels, up_weights, mid_weights, final_weights):
    result = []
    up_offset = 0
    down_offset = 0
    mid_count = 0
    if source_id > 0:
        lifted = jnp.dot(up_weights[source_id][module_id], source.reshape(source.shape[0], -1), preferred_element_type=jnp.float32)
    for target in range(4):
        if target == source_id:
            result.append(source)
        elif target < source_id:
            part = lifted[up_offset:up_offset + channels[target]].astype(jnp.bfloat16)
            up_offset = up_offset + channels[target]
            part = part.reshape(channels[target], source.shape[1], source.shape[2])
            factor = 2 ** (source_id - target)
            part = jnp.repeat(jnp.repeat(part, factor, axis=1), factor, axis=2)
            result.append(part)
        else:
            value = source
            for step_id in range(target - source_id - 1):
                value = jax.nn.relu(convolve(value, mid_weights[source_id][module_id, mid_count], 2)).astype(jnp.bfloat16)
                mid_count = mid_count + 1
            rows_used = final_weights[source_id][module_id, down_offset:down_offset + channels[target]]
            down_offset = down_offset + channels[target]
            result.append(convolve(value, rows_used, 2).astype(jnp.bfloat16))
    return result


def reference(feat0, feat1, feat2, feat3, block_w0, block_w1, block_w2, block_w3, block_b0, block_b1, block_b2, block_b3, up_w1, up_w2, up_w3, down_mid0, down_mid1, down_fin0, down_fin1, down_fin2):
    features = [feat0, feat1, feat2, feat3]
    block_weights = (block_w0, block_w1, block_w2, block_w3)
    block_biases = (block_b0, block_b1, block_b2, block_b3)
    up_weights = (None, up_w1, up_w2, up_w3)
    mid_weights = (down_mid0, down_mid1, None, None)
    final_weights = (down_fin0, down_fin1, down_fin2, None)
    channels = [feature.shape[0] for feature in features]
    for module_id in range(MODULES):
        sources = []
        for branch_id in range(4):
            source = features[branch_id]
            for block_id in range(BLOCKS):
                first_conv = (module_id * BLOCKS + block_id) * 2
                source = residual_block(source, block_weights[branch_id][first_conv], block_biases[branch_id][first_conv], block_weights[branch_id][first_conv + 1], block_biases[branch_id][first_conv + 1])
            sources.append(source)
        totals = [jnp.zeros(feature.shape, jnp.float32) for feature in features]
        for source_id in range(4):
            term_list = joining_terms(sources[source_id], source_id, module_id, channels, up_weights, mid_weights, final_weights)
            totals = [running + term.astype(jnp.float32) for running, term in zip(totals, term_list)]
        features = [jax.nn.relu(running).astype(jnp.bfloat16) for running in totals]
    return (features[0], features[1], features[2], features[3])
```

```python
import jax
import jax.numpy as jnp
from jax import lax
from jax.sharding import PartitionSpec as P


def neighbour(x, axis, by):
    devices = lax.axis_size(axis)
    pairs = [(i, i + by) for i in range(devices) if 0 <= i + by < devices]
    return lax.ppermute(x, axis, pairs)


def with_halo(x, low, high):
    rows = x.shape[0]
    above = neighbour(x[rows - low :], "ty", 1)
    below = neighbour(x[:high], "ty", -1)
    x = jnp.concatenate([above, x, below], axis=0)
    cols = x.shape[1]
    left = neighbour(jnp.swapaxes(x[:, cols - low :], 0, 1), "tx", 1)
    right = neighbour(jnp.swapaxes(x[:, :high], 0, 1), "tx", -1)
    return jnp.concatenate([jnp.swapaxes(left, 0, 1), x, jnp.swapaxes(right, 0, 1)], axis=1)


def inside(rows, cols, low, high):
    row_at = lax.axis_index("ty") * rows + jnp.arange(-low, rows + high, dtype=jnp.int32)
    col_at = lax.axis_index("tx") * cols + jnp.arange(-low, cols + high, dtype=jnp.int32)
    row_ok = (row_at >= 0) & (row_at < rows * lax.axis_size("ty"))
    col_ok = (col_at >= 0) & (col_at < cols * lax.axis_size("tx"))
    return (row_ok[:, None] & col_ok[None, :])[:, :, None]


def conv(x, weight, stride):
    out, depth = weight.shape[0], x.shape[2]
    kernel = weight.reshape(out, 3, 3, depth)
    return lax.conv_general_dilated(
        x[None],
        kernel,
        (stride, stride),
        "VALID",
        dimension_numbers=("NHWC", "OHWI", "NHWC"),
        preferred_element_type=jnp.float32,
    )[0]


def up2(x):
    rows, cols, depth = x.shape
    x = jnp.broadcast_to(x[:, None, :, None, :], (rows, 2, cols, 2, depth))
    return x.reshape(2 * rows, 2 * cols, depth)


def rounded(x):
    return x.astype(jnp.bfloat16)


def per_device(
    feat0,
    feat1,
    feat2,
    feat3,
    block_w0,
    block_w1,
    block_w2,
    block_w3,
    block_b0,
    block_b1,
    block_b2,
    block_b3,
    up_w1,
    up_w2,
    up_w3,
    down_mid0,
    down_mid1,
    down_fin0,
    down_fin1,
    down_fin2,
):
    feats = (feat0, feat1, feat2, feat3)
    weights = (block_w0, block_w1, block_w2, block_w3)
    biases = (block_b0, block_b1, block_b2, block_b3)
    channels = [f.shape[0] for f in feats]
    sizes = [f.shape[1:] for f in feats]
    rims = (7, 3, 1, 0)

    wide = []
    for b in range(4):
        rows, cols = sizes[b]
        rim = rims[b]
        x = with_halo(jnp.transpose(feats[b], (1, 2, 0)), rim + 2, 2)
        h = jax.nn.relu(conv(x, weights[b][0], 1) + biases[b][0])
        h = rounded(jnp.where(inside(rows, cols, rim + 1, 1), h, 0.0))
        core = x[2:-2, 2:-2].astype(jnp.float32)
        a = jax.nn.relu(core + conv(h, weights[b][1], 1) + biases[b][1])
        wide.append(rounded(jnp.where(inside(rows, cols, rim, 0), a, 0.0)))

    def ring(v, level, rim):
        rows, cols = sizes[level]
        return rounded(jnp.where(inside(rows, cols, rim, 0), jax.nn.relu(v), 0.0))

    own = [wide[b][rims[b] :, rims[b] :] for b in range(4)]
    c0, c1, c2, c3 = channels

    first = jnp.concatenate([down_fin0[0, :c1], down_mid0[0, 0], down_mid0[0, 1]], axis=0)
    step = conv(wide[0], first, 2)
    term01 = rounded(step[3:, 3:, :c1])
    v02 = ring(step[2:, 2:, c1 : c1 + c0], 1, 1)
    v03 = ring(step[:, :, c1 + c0 :], 1, 3)
    term02 = rounded(conv(v02, down_fin0[0, c1 : c1 + c2], 2))
    v03 = ring(conv(v03, down_mid0[0, 2], 2), 2, 1)
    term03 = rounded(conv(v03, down_fin0[0, c1 + c2 :], 2))

    second = jnp.concatenate([down_fin1[0, :c2], down_mid1[0, 0]], axis=0)
    step = conv(wide[1], second, 2)
    term12 = rounded(step[1:, 1:, :c2])
    v13 = ring(step[:, :, c2:], 2, 1)
    term13 = rounded(conv(v13, down_fin1[0, c2:], 2))
    term23 = rounded(conv(wide[2], down_fin2[0], 2))

    def lift(x, weight):
        return rounded(
            lax.dot_general(x, weight, (((2,), (1,)), ((), ())), preferred_element_type=jnp.float32)
        )

    up1 = lift(own[1], up_w1[0])
    up2_all = lift(own[2], up_w2[0])
    up3_all = lift(own[3], up_w3[0])

    def f32(x):
        return x.astype(jnp.float32)

    from3 = up2(f32(up3_all))
    to2 = from3[:, :, c0 + c1 :]
    from32 = up2(from3[:, :, : c0 + c1] + f32(up2_all))
    to1 = from32[:, :, c0:]
    to0 = up2(from32[:, :, :c0] + f32(up1))

    totals = (
        f32(own[0]) + to0,
        f32(own[1]) + to1 + f32(term01),
        f32(own[2]) + to2 + f32(term02) + f32(term12),
        f32(own[3]) + f32(term03) + f32(term13) + f32(term23),
    )
    return tuple(jnp.transpose(rounded(jax.nn.relu(t)), (2, 0, 1)) for t in totals)


def solution(mesh):
    tiled = P(None, "ty", "tx")
    return jax.shard_map(
        per_device,
        mesh=mesh,
        in_specs=(tiled,) * 4 + (P(),) * 16,
        out_specs=(tiled,) * 4,
        check_vma=False,
    )
```

```python
import functools

import jax
import jax.numpy as jnp
import numpy as np
from jax import lax
from jax.experimental import pallas as pl
from jax.experimental.pallas import tpu as pltpu
from jax.sharding import PartitionSpec as P


RIMS = (7, 3, 1, 0)
LEAD = (16, 8, 8, 16)
TAIL = (16, 8, 4, 4)


def up128(n):
    return -(-n // 128) * 128


def neighbour(x, axis, by):
    devices = lax.axis_size(axis)
    pairs = [(i, i + by) for i in range(devices) if 0 <= i + by < devices]
    return lax.ppermute(x, axis, pairs)


def with_halo(x, low, high):
    rows, cols = x.shape[1:]
    above = neighbour(x[:, rows - low :], "ty", 1)
    below = neighbour(x[:, :high], "ty", -1)
    x = jnp.concatenate([above, x, below], axis=1)
    left = neighbour(jnp.transpose(x[:, :, cols - low :], (2, 0, 1)), "tx", 1)
    right = neighbour(jnp.transpose(x[:, :, :high], (2, 0, 1)), "tx", -1)
    left, right = jnp.transpose(left, (1, 2, 0)), jnp.transpose(right, (1, 2, 0))
    return jnp.concatenate([left, x, right], axis=2)


def lanes_of(level, rows):
    return (90, 44, 32, 40)[level] + rows - (64, 32, 16, 8)[level]


def flat(x, level, rows, cols):
    low = RIMS[level] + 2
    pitch = 2 * cols
    x = jnp.pad(x, ((0, 0), (0, 0), (0, pitch - x.shape[2])))
    x = x.reshape(x.shape[0], -1)
    front = (LEAD[level] - low) * pitch - low
    total = lanes_of(level, rows) * pitch
    return jnp.pad(x, ((0, 0), (front, total - front - x.shape[1])))


def picks(level, pitch):
    small = pitch // 2
    at = np.arange(512)
    out = np.arange(128)
    row, col = out // small, out % small
    source = (2 * row + (col >= small - TAIL[level + 1])) * pitch + 2 * col
    down = (at[:, None] == source[None, :]).astype(np.float32)
    row, col = at // pitch, at % pitch
    source = (row // 2) * small + col // 2
    up = (out[:, None] == source[None, :]).astype(np.float32)
    return down, up


def body(sizes, channels, *refs):
    xs, ws, bs = refs[0:4], refs[4:8], refs[8:12]
    up1, up2, up3, mid0, mid1, fin0, fin1, fin2 = refs[12:20]
    downs, ups = refs[20:23], refs[23:26]
    outs = refs[26:30]
    taps, hs, maps = refs[30:34], refs[34:38], refs[38:42]
    t01, v02, v03, t02, t12, v03b, v13, s1 = refs[42:50]
    f32, bf16 = jnp.float32, jnp.bfloat16
    c0, c1, c2, c3 = channels
    pitch = [2 * cols for _, cols in sizes]
    places = [LEAD[l] * pitch[l] for l in range(4)]
    inner = [sizes[l][0] * pitch[l] for l in range(4)]

    def mask(level, start, n):
        rows, cols = sizes[level]
        f = lax.broadcasted_iota(jnp.int32, (1, n), 1) + (start + TAIL[level])
        r = f // pitch[level] - LEAD[level] + lax.axis_index("ty") * rows
        c = f % pitch[level] - TAIL[level] + lax.axis_index("tx") * cols
        ok = (r >= 0) & (r < rows * lax.axis_size("ty"))
        return ok & (c >= 0) & (c < cols * lax.axis_size("tx"))

    def dot(a, b):
        return lax.dot_general(a, b, (((1,), (0,)), ((), ())), preferred_element_type=f32)

    def fill(level, source):
        depth, total = source.shape
        to = taps[level]

        def step(i, _):
            at = pl.multiple_of(i * 16, 16)
            x = source[pl.ds(at, 16), :].astype(f32)
            for t in range(9):
                by = (t // 3 - 1) * pitch[level] + t % 3 - 1
                y = pltpu.roll(x, (-by) % total, 1) if by else x
                to[pl.ds(pl.multiple_of(t * depth + at, 16), 16), :] = y.astype(bf16)
            return 0

        lax.fori_loop(0, depth // 16, step, 0)

    def chunks(start, end, size, run):
        count = -(-(end - start) // size)

        def step(i, _):
            run(pl.multiple_of(start + i * size, 128))
            return 0

        if count == 1:
            run(start)
        else:
            lax.fori_loop(0, count, step, 0)

    for ref in (*hs, *maps[:3], v02, v03, v03b, v13):
        ref[...] = jnp.zeros_like(ref)

    for l in range(4):
        rim = RIMS[l]
        fill(l, xs[l])
        begin = (LEAD[l] - rim - 2) * pitch[l] // 128 * 128
        end = up128((LEAD[l] + sizes[l][0] + 1) * pitch[l])
        size = (1024, 512, 256, end - begin)[l]

        def first(at, l=l, size=size):
            y = dot(ws[l][0], taps[l][:, pl.ds(at, size)]) + bs[l][:, 0:1]
            y = jnp.where(mask(l, at, size), jnp.maximum(y, 0.0), 0.0)
            hs[l][:, pl.ds(at, size)] = y.astype(bf16)

        chunks(begin, end, size, first)
        fill(l, hs[l])
        begin = (LEAD[l] - rim - 1) * pitch[l] // 128 * 128
        end = places[l] + inner[l]
        if l == 3:
            begin = places[l]
        size = (1024, 768, 128, end - begin)[l]

        def second(at, l=l, size=size):
            y = dot(ws[l][1], taps[l][:, pl.ds(at, size)]) + bs[l][:, 1:2]
            y = jnp.maximum(y + xs[l][:, pl.ds(at, size)].astype(f32), 0.0)
            maps[l][:, pl.ds(at, size)] = jnp.where(mask(l, at, size), y, 0.0).astype(bf16)

        chunks(begin, end, size, second)

    def shrink(y, level):
        return dot(y.astype(bf16), downs[level][...])

    fill(0, maps[0])

    def run(at):
        source = pl.multiple_of(at * 4, 512)
        cols = taps[0][:, pl.ds(source, 512)]
        ok = mask(1, at, 128)
        y = dot(fin0[0, 0:c1, :], cols)
        t01[:, pl.ds(at, 128)] = shrink(y, 0).astype(bf16)
        for k, to in ((0, v02), (1, v03)):
            y = jnp.maximum(dot(mid0[0, k], cols), 0.0)
            to[:, pl.ds(at, 128)] = jnp.where(ok, shrink(y, 0), 0.0).astype(bf16)

    chunks((LEAD[1] - 4) * pitch[1], places[1] + inner[1], 128, run)

    def level1(source, weight, to, rim):
        depth = source.shape[0]
        fill(1, source)

        def run(at):
            cols = taps[1][0 : 9 * depth, pl.ds(pl.multiple_of(at * 4 - 512, 512), 512)]
            y = dot(weight(), cols)
            if rim:
                y = shrink(jnp.maximum(y, 0.0), 1)
                y = jnp.where(mask(2, at, 128), y, 0.0)
            else:
                y = shrink(y, 1)
            to[:, pl.ds(at, 128)] = y.astype(bf16)

        start = places[2] - (128 if rim else 0)
        chunks(start, places[2] + inner[2], 128, run)
        return run, start

    level1(v02, lambda: fin0[0, c1 : c1 + c2, :], t02, 0)
    level1(v03, lambda: mid0[0, 2], v03b, 1)
    level1(maps[1], lambda: fin1[0, 0:c2, :], t12, 0)
    chunked = places[2]

    def run13(at):
        cols = taps[1][:, pl.ds(pl.multiple_of(at * 4 - 512, 512), 512)]
        y = shrink(jnp.maximum(dot(mid1[0, 0], cols), 0.0), 1)
        v13[:, pl.ds(at, 128)] = jnp.where(mask(2, at, 128), y, 0.0).astype(bf16)

    chunks(chunked - 128, chunked + inner[2], 128, run13)

    total3 = maps[3][:, places[3] : places[3] + inner[3]].astype(f32)
    for source, weight in (
        (v03b, lambda: fin0[0, c1 + c2 : c1 + c2 + c3, :]),
        (v13, lambda: fin1[0, c2 : c2 + c3, :]),
        (maps[2], lambda: fin2[0]),
    ):
        fill(2, source)
        y = dot(weight(), taps[2][0 : 9 * source.shape[0], places[2] : places[2] + inner[2]])
        total3 = total3 + shrink(y, 2).astype(bf16).astype(f32)
    outs[3][...] = jnp.maximum(total3, 0.0).astype(bf16)

    u3 = dot(up3[0], maps[3][:, places[3] : places[3] + inner[3]]).astype(bf16)
    u3 = dot(u3, ups[2][...]).astype(bf16)
    a2 = maps[2][:, places[2] : places[2] + inner[2]]
    u2 = dot(up2[0], a2).astype(bf16)
    total2 = a2.astype(f32) + u3[c0 + c1 :].astype(f32)
    total2 = total2 + t02[:, places[2] : places[2] + inner[2]].astype(f32)
    total2 = total2 + t12[:, places[2] : places[2] + inner[2]].astype(f32)
    outs[2][...] = jnp.maximum(total2, 0.0).astype(bf16)
    pair = jnp.concatenate([u3[: c0 + c1], u2], axis=0)
    for k in range(inner[2] // 128):
        y = dot(pair[:, 128 * k : 128 * (k + 1)], ups[1][...]).astype(bf16)
        at = 512 * k
        place = places[1] + at
        a1 = maps[1][:, place : place + 512]
        total1 = a1.astype(f32) + t01[:, place : place + 512].astype(f32)
        total1 = total1 + y[c0 : c0 + c1].astype(f32) + y[c0 + c1 + c0 :].astype(f32)
        outs[1][:, at : at + 512] = jnp.maximum(total1, 0.0).astype(bf16)
        s1[0:c0, at : at + 512] = y[0:c0]
        s1[c0 : 2 * c0, at : at + 512] = y[c0 + c1 : 2 * c0 + c1]
        s1[2 * c0 :, at : at + 512] = dot(up1[0], a1).astype(bf16)

    def last(at):
        y = dot(s1[:, pl.ds(at, 128)], ups[0][...])
        to = pl.multiple_of(at * 4, 512)
        total0 = maps[0][:, pl.ds(pl.multiple_of(places[0] + to, 128), 512)].astype(f32)
        total0 = total0 + y[:c0] + y[c0 : 2 * c0] + y[2 * c0 :]
        outs[0][:, pl.ds(to, 512)] = jnp.maximum(total0, 0.0).astype(bf16)

    chunks(0, inner[1], 128, last)


def per_device(*args):
    feats, weights, biases, rest = args[0:4], args[4:8], args[8:12], args[12:20]
    bf16 = jnp.bfloat16
    channels = [f.shape[0] for f in feats]
    sizes = [f.shape[1:] for f in feats]
    c0, c1, c2, c3 = channels
    xs = []
    for l in range(4):
        x = with_halo(feats[l], RIMS[l] + 2, 2)
        xs.append(flat(x, l, *sizes[l]))
    made = [picks(l, 2 * sizes[l][1]) for l in range(3)]
    downs = [jnp.asarray(d, bf16) for d, _ in made]
    ups = [jnp.asarray(u, bf16) for _, u in made]
    total = [x.shape[1] for x in xs]
    vmem = pltpu.VMEM
    scratch = [vmem((9 * channels[l], total[l]), bf16) for l in range(4)]
    scratch += [vmem((channels[l], total[l]), bf16) for l in range(4)] * 2
    for depth, level in ((c1, 1), (c0, 1), (c0, 1), (c2, 2), (c2, 2), (c0, 2), (c1, 2)):
        scratch.append(vmem((depth, total[level]), bf16))
    scratch.append(vmem((3 * c0, sizes[1][0] * 2 * sizes[1][1]), bf16))
    whole = pl.BlockSpec(memory_space=pltpu.VMEM)
    outs = pl.pallas_call(
        functools.partial(body, sizes, channels),
        out_shape=[
            jax.ShapeDtypeStruct((channels[l], 2 * sizes[l][0] * sizes[l][1]), bf16)
            for l in range(4)
        ],
        in_specs=[whole] * 26,
        out_specs=[whole] * 4,
        scratch_shapes=scratch,
        compiler_params=pltpu.CompilerParams(vmem_limit_bytes=67043328),
    )(*xs, *weights, *[b.T for b in biases], *rest, *downs, *ups)
    return tuple(
        o.reshape(channels[l], sizes[l][0], 2 * sizes[l][1])[:, :, : sizes[l][1]]
        for l, o in enumerate(outs)
    )


def solution(mesh):
    tiled = P(None, "ty", "tx")
    return jax.shard_map(
        per_device,
        mesh=mesh,
        in_specs=(tiled,) * 4 + (P(),) * 16,
        out_specs=(tiled,) * 4,
        check_vma=False,
    )
```

```python
import functools

import jax
import jax.numpy as jnp
import numpy as np
from jax import lax
from jax.experimental import pallas as pl
from jax.experimental.pallas import tpu as pltpu
from jax.sharding import PartitionSpec as P


RIMS = (7, 3, 1, 0)
LEAD = (16, 8, 8, 16)
TAIL = (16, 8, 4, 4)


def up128(n):
    return -(-n // 128) * 128


def neighbour(x, axis, by):
    devices = lax.axis_size(axis)
    pairs = [(i, i + by) for i in range(devices) if 0 <= i + by < devices]
    return lax.ppermute(x, axis, pairs)


def sent(slabs, axis, by):
    deep = max(s.shape[0] for s in slabs)
    long = max(s.shape[2] for s in slabs)
    padded = [jnp.pad(s, ((0, deep - s.shape[0]), (0, 0), (0, long - s.shape[2]))) for s in slabs]
    moved = neighbour(jnp.concatenate(padded, axis=1), axis, by)
    parts, at = [], 0
    for s in slabs:
        parts.append(moved[: s.shape[0], at : at + s.shape[1], : s.shape[2]])
        at = at + s.shape[1]
    return parts


def with_halos(xs, lows, high):
    for axis, dim in (("ty", 1), ("tx", 2)):
        last, first = [], []
        for x, low in zip(xs, lows):
            end = x.shape[dim]
            last.append(jnp.moveaxis(lax.slice_in_dim(x, end - low, end, axis=dim), dim, 0))
            first.append(jnp.moveaxis(lax.slice_in_dim(x, 0, high, axis=dim), dim, 0))
        before = sent(last[:2], axis, 1) + sent(last[2:], axis, 1)
        after = sent(first, axis, -1)
        xs = [
            jnp.concatenate([jnp.moveaxis(b, 0, dim), x, jnp.moveaxis(a, 0, dim)], axis=dim)
            for b, x, a in zip(before, xs, after)
        ]
    return xs


def lanes_of(level, rows):
    return (90, 44, 32, 40)[level] + rows - (64, 32, 16, 8)[level]


def flat(x, level, rows, cols):
    low = RIMS[level] + 2
    pitch = 2 * cols
    x = jnp.pad(x, ((0, 0), (0, 0), (0, pitch - x.shape[2])))
    x = x.reshape(x.shape[0], -1)
    front = (LEAD[level] - low) * pitch - low
    total = lanes_of(level, rows) * pitch
    return jnp.pad(x, ((0, 0), (front, total - front - x.shape[1])))


def picks(level, pitch):
    small = pitch // 2
    at = np.arange(512)
    out = np.arange(128)
    row, col = out // small, out % small
    source = (2 * row + (col >= small - TAIL[level + 1])) * pitch + 2 * col
    down = (at[:, None] == source[None, :]).astype(np.float32)
    row, col = at // pitch, at % pitch
    source = (row // 2) * small + col // 2
    up = (out[:, None] == source[None, :]).astype(np.float32)
    return down, up


def body(sizes, channels, *refs):
    xs, ws, bs = refs[0:4], refs[4:8], refs[8:12]
    up1, up2, up3, mid0, mid1, fin0, fin1, fin2 = refs[12:20]
    downs, ups = refs[20:23], refs[23:26]
    outs = refs[26:30]
    taps, hs, maps = refs[30:34], refs[34:38], refs[38:42]
    t01, v02, v03, t02, t12, v03b, v13, s1 = refs[42:50]
    f32, bf16 = jnp.float32, jnp.bfloat16
    c0, c1, c2, c3 = channels
    pitch = [2 * cols for _, cols in sizes]
    places = [LEAD[l] * pitch[l] for l in range(4)]
    inner = [sizes[l][0] * pitch[l] for l in range(4)]

    def mask(level, start, n):
        rows, cols = sizes[level]
        f = lax.broadcasted_iota(jnp.int32, (1, n), 1) + (start + TAIL[level])
        r = f // pitch[level] - LEAD[level] + lax.axis_index("ty") * rows
        c = f % pitch[level] - TAIL[level] + lax.axis_index("tx") * cols
        ok = (r >= 0) & (r < rows * lax.axis_size("ty"))
        return ok & (c >= 0) & (c < cols * lax.axis_size("tx"))

    def dot(a, b):
        return lax.dot_general(a, b, (((1,), (0,)), ((), ())), preferred_element_type=f32)

    def fill(level, source):
        depth, total = source.shape
        to = taps[level]

        def step(i, _):
            at = pl.multiple_of(i * 16, 16)
            x = source[pl.ds(at, 16), :].astype(f32)
            for t in range(9):
                by = (t // 3 - 1) * pitch[level] + t % 3 - 1
                y = pltpu.roll(x, (-by) % total, 1) if by else x
                to[pl.ds(pl.multiple_of(t * depth + at, 16), 16), :] = y.astype(bf16)
            return 0

        lax.fori_loop(0, depth // 16, step, 0)

    def chunks(start, end, size, run):
        count = -(-(end - start) // size)

        def step(i, _):
            run(pl.multiple_of(start + i * size, 128))
            return 0

        if count == 1:
            run(start)
        else:
            lax.fori_loop(0, count, step, 0)

    for ref in (*hs, *maps[:3], v02, v03, v03b, v13):
        ref[...] = jnp.zeros_like(ref)

    for l in range(4):
        rim = RIMS[l]
        fill(l, xs[l])
        begin = (LEAD[l] - rim - 2) * pitch[l] // 128 * 128
        end = up128((LEAD[l] + sizes[l][0] + 1) * pitch[l])
        size = (1024, 512, 256, end - begin)[l]

        def first(at, l=l, size=size):
            y = dot(ws[l][0], taps[l][:, pl.ds(at, size)]) + bs[l][:, 0:1]
            y = jnp.where(mask(l, at, size), jnp.maximum(y, 0.0), 0.0)
            hs[l][:, pl.ds(at, size)] = y.astype(bf16)

        chunks(begin, end, size, first)
        fill(l, hs[l])
        begin = (LEAD[l] - rim - 1) * pitch[l] // 128 * 128
        end = places[l] + inner[l]
        if l == 3:
            begin = places[l]
        size = (1024, 768, 128, end - begin)[l]

        def second(at, l=l, size=size):
            y = dot(ws[l][1], taps[l][:, pl.ds(at, size)]) + bs[l][:, 1:2]
            y = jnp.maximum(y + xs[l][:, pl.ds(at, size)].astype(f32), 0.0)
            maps[l][:, pl.ds(at, size)] = jnp.where(mask(l, at, size), y, 0.0).astype(bf16)

        chunks(begin, end, size, second)

    def shrink(y, level):
        return dot(y.astype(bf16), downs[level][...])

    fill(0, maps[0])

    def run(at):
        source = pl.multiple_of(at * 4, 512)
        cols = taps[0][:, pl.ds(source, 512)]
        ok = mask(1, at, 128)
        y = dot(fin0[0, 0:c1, :], cols)
        t01[:, pl.ds(at, 128)] = shrink(y, 0).astype(bf16)
        for k, to in ((0, v02), (1, v03)):
            y = jnp.maximum(dot(mid0[0, k], cols), 0.0)
            to[:, pl.ds(at, 128)] = jnp.where(ok, shrink(y, 0), 0.0).astype(bf16)

    chunks((LEAD[1] - 4) * pitch[1], places[1] + inner[1], 128, run)

    def level1(source, weight, to, rim):
        depth = source.shape[0]
        fill(1, source)

        def run(at):
            cols = taps[1][0 : 9 * depth, pl.ds(pl.multiple_of(at * 4 - 512, 512), 512)]
            y = dot(weight(), cols)
            if rim:
                y = shrink(jnp.maximum(y, 0.0), 1)
                y = jnp.where(mask(2, at, 128), y, 0.0)
            else:
                y = shrink(y, 1)
            to[:, pl.ds(at, 128)] = y.astype(bf16)

        start = places[2] - (128 if rim else 0)
        chunks(start, places[2] + inner[2], 128, run)
        return run, start

    level1(v02, lambda: fin0[0, c1 : c1 + c2, :], t02, 0)
    level1(v03, lambda: mid0[0, 2], v03b, 1)
    level1(maps[1], lambda: fin1[0, 0:c2, :], t12, 0)
    chunked = places[2]

    def run13(at):
        cols = taps[1][:, pl.ds(pl.multiple_of(at * 4 - 512, 512), 512)]
        y = shrink(jnp.maximum(dot(mid1[0, 0], cols), 0.0), 1)
        v13[:, pl.ds(at, 128)] = jnp.where(mask(2, at, 128), y, 0.0).astype(bf16)

    chunks(chunked - 128, chunked + inner[2], 128, run13)

    total3 = maps[3][:, places[3] : places[3] + inner[3]].astype(f32)
    for source, weight in (
        (v03b, lambda: fin0[0, c1 + c2 : c1 + c2 + c3, :]),
        (v13, lambda: fin1[0, c2 : c2 + c3, :]),
        (maps[2], lambda: fin2[0]),
    ):
        fill(2, source)
        y = dot(weight(), taps[2][0 : 9 * source.shape[0], places[2] : places[2] + inner[2]])
        total3 = total3 + shrink(y, 2).astype(bf16).astype(f32)
    outs[3][...] = jnp.maximum(total3, 0.0).astype(bf16)

    u3 = dot(up3[0], maps[3][:, places[3] : places[3] + inner[3]]).astype(bf16)
    u3 = dot(u3, ups[2][...]).astype(bf16)
    a2 = maps[2][:, places[2] : places[2] + inner[2]]
    u2 = dot(up2[0], a2).astype(bf16)
    total2 = a2.astype(f32) + u3[c0 + c1 :].astype(f32)
    total2 = total2 + t02[:, places[2] : places[2] + inner[2]].astype(f32)
    total2 = total2 + t12[:, places[2] : places[2] + inner[2]].astype(f32)
    outs[2][...] = jnp.maximum(total2, 0.0).astype(bf16)
    pair = jnp.concatenate([u3[: c0 + c1], u2], axis=0)
    for k in range(inner[2] // 128):
        y = dot(pair[:, 128 * k : 128 * (k + 1)], ups[1][...]).astype(bf16)
        at = 512 * k
        place = places[1] + at
        a1 = maps[1][:, place : place + 512]
        total1 = a1.astype(f32) + t01[:, place : place + 512].astype(f32)
        total1 = total1 + y[c0 : c0 + c1].astype(f32) + y[c0 + c1 + c0 :].astype(f32)
        outs[1][:, at : at + 512] = jnp.maximum(total1, 0.0).astype(bf16)
        s1[0:c0, at : at + 512] = y[0:c0]
        s1[c0 : 2 * c0, at : at + 512] = y[c0 + c1 : 2 * c0 + c1]
        s1[2 * c0 :, at : at + 512] = dot(up1[0], a1).astype(bf16)

    def last(at):
        y = dot(s1[:, pl.ds(at, 128)], ups[0][...])
        to = pl.multiple_of(at * 4, 512)
        total0 = maps[0][:, pl.ds(pl.multiple_of(places[0] + to, 128), 512)].astype(f32)
        total0 = total0 + y[:c0] + y[c0 : 2 * c0] + y[2 * c0 :]
        outs[0][:, pl.ds(to, 512)] = jnp.maximum(total0, 0.0).astype(bf16)

    chunks(0, inner[1], 128, last)


def per_device(*args):
    feats, weights, biases, rest = args[0:4], args[4:8], args[8:12], args[12:20]
    bf16 = jnp.bfloat16
    channels = [f.shape[0] for f in feats]
    sizes = [f.shape[1:] for f in feats]
    c0, c1, c2, c3 = channels
    xs = with_halos(feats, [rim + 2 for rim in RIMS], 2)
    xs = [flat(x, l, *sizes[l]) for l, x in enumerate(xs)]
    made = [picks(l, 2 * sizes[l][1]) for l in range(3)]
    downs = [jnp.asarray(d, bf16) for d, _ in made]
    ups = [jnp.asarray(u, bf16) for _, u in made]
    total = [x.shape[1] for x in xs]
    vmem = pltpu.VMEM
    scratch = [vmem((9 * channels[l], total[l]), bf16) for l in range(4)]
    scratch += [vmem((channels[l], total[l]), bf16) for l in range(4)] * 2
    for depth, level in ((c1, 1), (c0, 1), (c0, 1), (c2, 2), (c2, 2), (c0, 2), (c1, 2)):
        scratch.append(vmem((depth, total[level]), bf16))
    scratch.append(vmem((3 * c0, sizes[1][0] * 2 * sizes[1][1]), bf16))
    whole = pl.BlockSpec(memory_space=pltpu.VMEM)
    outs = pl.pallas_call(
        functools.partial(body, sizes, channels),
        out_shape=[
            jax.ShapeDtypeStruct((channels[l], 2 * sizes[l][0] * sizes[l][1]), bf16)
            for l in range(4)
        ],
        in_specs=[whole] * 26,
        out_specs=[whole] * 4,
        scratch_shapes=scratch,
        compiler_params=pltpu.CompilerParams(vmem_limit_bytes=67043328),
    )(*xs, *weights, *[b.T for b in biases], *rest, *downs, *ups)
    return tuple(
        o.reshape(channels[l], sizes[l][0], 2 * sizes[l][1])[:, :, : sizes[l][1]]
        for l, o in enumerate(outs)
    )


def solution(mesh):
    tiled = P(None, "ty", "tx")
    return jax.shard_map(
        per_device,
        mesh=mesh,
        in_specs=(tiled,) * 4 + (P(),) * 16,
        out_specs=(tiled,) * 4,
        check_vma=False,
    )
```
